32 devices in a mesh: ex: 8 (over y, x, core), co: 4 (over z).
Axes of the slice: x: 2, y: 2, z: 4, core: 2. Of those that a mesh axis runs over, the one named last changes fastest.
Arguments:
- train_grads: float32 [8192, 32768], P('ex', 'co')
- queries: float32 [1024, 32768], P('ex', 'co'), may hold values from -6 to 6
- module_ids: int32 [8], replicated, may hold values from 0 to 223
- module_scale: float32 [224], replicated, may hold values from 0.3 to 3
- example_ids: int32 [8192], P('ex'), may hold values from 0 to 8191, as said below
Outputs:
- influence: float32 [1024, 8192], P('co', 'ex')
The draws below stay inside these ranges and needn't reach their ends.
Inputs may be any that keep to these rules, and one draw needn't show every extreme that they name: `example_ids`: the examples of block s of 1024 rows carry the ids s * 1024 to (s + 1) * 1024 - 1, each once.
All inputs are finite; a program needn't handle non-finite values.
Results may differ from the reference program's by a relative error of at most 0.00008.
Values sent between devices are 32-bit elements; how exact they have to be, the bound alone decides.
A program may use at most 128 MiB of HBM per device.

```python
import math
import jax
import jax.numpy as jnp
from jax import lax

PROJ = 4096
TOTAL_MODS = 224
MODS = 8
E_DEV = 1024
QUERIES = 1024
COORD = 32768
EXAMPLES = 8192


def draw_train_grads(key, part):
    key_row, key_col, key_main = jax.random.split(key, 3)
    row_scale = jnp.exp(jax.random.uniform(key_row, (EXAMPLES, 1), jnp.float32) * jnp.log(10.0))
    col_scale = jnp.exp(jax.random.uniform(key_col, (1, COORD), jnp.float32) * jnp.log(10.0))
    growth = (jnp.arange(COORD, dtype=jnp.float32) / COORD)[None, :]
    growth = jnp.exp(growth * jnp.log(3.0))
    entries = jax.random.normal(key_main, (EXAMPLES, COORD), jnp.float32)
    return (entries * row_scale * col_scale * growth / jnp.sqrt(jnp.float32(COORD))).astype(jnp.float32)


def shuffle_block(block_key):
    return jax.random.permutation(block_key, E_DEV)


def draw_example_ids(key, part):
    shards = EXAMPLES // E_DEV
    shard_keys = jax.random.split(jax.random.fold_in(key, 7), shards)
    shuffled = jax.vmap(shuffle_block)(shard_keys).astype(jnp.int32)
    offsets = (jnp.arange(shards, dtype=jnp.int32) * E_DEV)[:, None]
    return (shuffled + offsets).reshape(-1).astype(jnp.int32)


def place_ends(drawn, stream_key, least, high):
    extent = drawn.shape
    spot = [jax.random.randint(jax.random.fold_in(stream_key, axis), (), 0, extent[axis]) for axis in range(len(extent))]
    drawn = drawn.at[tuple(spot)].set(least)
    longest = extent.index(max(extent))
    spot[longest] = (spot[longest] + 1) % extent[longest]
    return drawn.at[tuple(spot)].set(high)


def with_spikes(values, key, source, target, blocks, factor):
    def block_of(dim):
        return (jnp.arange(values.shape[dim]) // (values.shape[dim] // blocks)).reshape((-1,) + (1,) * (values.ndim - 1 - dim))

    near = jax.random.permutation(key, blocks)[block_of(target)]
    second = (block_of(target) + blocks // 2) % blocks
    return jnp.where((block_of(source) == near) | (block_of(source) == second), factor * values, values)


def levels(stream_key, dims, cuts, low, largest):
    factor_of, own = 1.0, jax.random.fold_in(stream_key, 6)
    for dim, parts in cuts:
        draws = jnp.exp(jax.random.uniform(jax.random.fold_in(own, dim), (parts,), jnp.float32, low / len(cuts), largest / len(cuts)))
        factor_of = factor_of * jnp.repeat(draws, dims[dim] // parts).reshape([-1 if axis == dim else 1 for axis in range(len(dims))])
    return factor_of


def heavy_noise(stream_key, dims, width, bound, cuts, heavy, kind=jnp.bfloat16):
    array = width * jax.random.normal(stream_key, dims, jnp.float32)
    if cuts:
        array = array * levels(stream_key, dims, cuts, -0.22, 0.18)
    return jnp.clip(with_spikes(array, jax.random.fold_in(stream_key, 3), *heavy), -bound, bound).astype(kind)


def setup_inputs(seed: int = 0) -> dict:
    splits = jax.random.split(jax.random.key(seed), 6)
    return {
        "train_grads": draw_train_grads(jax.random.fold_in(splits[5], 71), 0),
        "queries": heavy_noise(splits[1], (QUERIES, COORD), 1.0, 6.0, ((0, 8), (1, 4)), (1, 0, 8, 2.0), jnp.float32),
        "module_ids": place_ends(jax.random.randint(splits[2], (MODS,), 0, TOTAL_MODS), jax.random.fold_in(splits[2], 1), 0, TOTAL_MODS - 1).astype(jnp.int32),
        "module_scale": jnp.clip(jnp.exp(jax.random.uniform(splits[3], (TOTAL_MODS,), jnp.float32, math.log(0.3), math.log(3.0))), 0.3, 3.0),
        "example_ids": draw_example_ids(jax.random.fold_in(splits[5], 71), 0),
    }


epsilon = 1e-06

def reference(train_grads, queries, module_ids, module_scale, example_ids):
    table_index = lax.iota(jnp.int32, module_scale.shape[0])
    picked = lax.optimization_barrier(jnp.sum(jnp.where(module_ids[:, None] == table_index[None, :], module_scale[None, :], jnp.zeros((), module_scale.dtype)), axis=1))
    position = lax.iota(jnp.int32, COORD)
    coord_scale = picked[(position // PROJ).astype(jnp.int32)]
    scaled = queries * coord_scale[None, :]
    squares = lax.optimization_barrier(jnp.sum(train_grads * train_grads, axis=1))
    inverse_norm = lax.rsqrt(squares + epsilon)
    raw_scores = lax.dot_general(scaled, train_grads, (((1,), (1,)), ((), ())), precision=lax.Precision.HIGHEST, preferred_element_type=jnp.float32)
    normed = raw_scores * inverse_norm[None, :]
    return jnp.zeros_like(normed).at[:, example_ids].set(normed)
```

```python
import functools

import jax
import jax.numpy as jnp
from jax import lax
from jax.experimental import pallas as pl
from jax.experimental.pallas import tpu as pltpu
from jax.sharding import PartitionSpec as P

PROJ = 4096
MESH = pl.DeviceIdType.MESH
PIECES = 4
CONTRACT_LAST = (((1,), (1,)), ((), ()))

epsilon = 1e-06


def kernel(n_ex, n_co, pieces, q_ref, g_ref, scale_ref, out_ref, buf,
           ghi, glo, stage, qhi, qlo, part, got, sq_own, sq_got,
           ring_send, ring_recv, sib_send, sib_recv, part_send, part_recv, sq_send, sq_recv, load_sem):
    chips = n_ex // 2
    half = chips // 2
    ex = lax.axis_index("ex")
    co = lax.axis_index("co")
    core = ex % 2

    def snake(pos):
        upper = pos // half
        return pos * (1 - upper) + upper * (half + chips - 1 - pos)

    pos = snake(ex // 2)

    def device_at(step):
        return snake((pos + step + chips) % chips) * 2 + core

    right = device_at(1)
    left = device_at(-1)
    sibling = ex + 1 - 2 * core
    rows = q_ref.shape[0] // pieces
    mid = rows // 2
    width = q_ref.shape[1]
    examples = g_ref.shape[0]
    owned = (n_ex // n_co) * rows

    barrier = pltpu.get_barrier_semaphore()
    for other in (right, left, sibling):
        pl.semaphore_signal(barrier, inc=1, device_id={"ex": other}, device_id_type=MESH)
    for k in range(1, n_co):
        pl.semaphore_signal(barrier, inc=1, device_id={"co": (co + k) % n_co}, device_id_type=MESH)
    pl.semaphore_wait(barrier, 3 + n_co - 1)

    def own_rows(s):
        return q_ref.at[pl.ds(pl.multiple_of(s * rows, rows), rows)]

    def ring_copy(way, d, s, arriving):
        back = d if arriving else d - 1
        origin = device_at(-back if way == 0 else back)
        if d == half and half > 1:
            span = pl.ds(way * mid, mid)
        else:
            span = pl.ds(0, rows)
        if d == 1 and not arriving:
            src = own_rows(s)
        else:
            src = buf.at[s, origin, span]
        return pltpu.make_async_remote_copy(
            src_ref=src,
            dst_ref=buf.at[s, origin, span],
            send_sem=ring_send.at[way, d - 1, s],
            recv_sem=ring_recv.at[way, d - 1, s],
            device_id={"ex": right if way == 0 else left},
            device_id_type=MESH,
        )

    def sibling_copy(off, s, arriving):
        origin = device_at(off)
        if arriving:
            origin = origin + 1 - 2 * core
        src = own_rows(s) if off == 0 and not arriving else buf.at[s, origin]
        return pltpu.make_async_remote_copy(
            src_ref=src,
            dst_ref=buf.at[s, origin],
            send_sem=sib_send.at[off, s],
            recv_sem=sib_recv.at[off, s],
            device_id={"ex": sibling},
            device_id_type=MESH,
        )

    def part_copy(k, s, arriving):
        owner = (co + k) % n_co
        return pltpu.make_async_remote_copy(
            src_ref=part.at[s, pl.ds(pl.multiple_of(owner * owned, owned), owned)],
            dst_ref=got.at[k - 1, s],
            send_sem=part_send.at[k - 1, s],
            recv_sem=part_recv.at[k - 1, s],
            device_id={"co": owner},
            device_id_type=MESH,
        )

    def sq_copy(k):
        return pltpu.make_async_remote_copy(
            src_ref=sq_own,
            dst_ref=sq_got.at[k - 1],
            send_sem=sq_send.at[k - 1],
            recv_sem=sq_recv.at[k - 1],
            device_id={"co": (co + k) % n_co},
            device_id_type=MESH,
        )

    def send_own(s):
        ring_copy(0, 1, s, False).start()
        ring_copy(1, 1, s, False).start()
        sibling_copy(0, s, False).start()

    send_own(0)
    send_own(1)

    tile = stage.shape[0] // 2
    tiles = examples // tile
    strip = min(512, width)

    def g_load(i):
        slot = i % 2
        return pltpu.make_async_copy(
            g_ref.at[pl.ds(pl.multiple_of(i * tile, tile), tile)],
            stage.at[pl.ds(pl.multiple_of(slot * tile, tile), tile)],
            load_sem.at[slot],
        )

    g_load(0).start()

    def split_tile(i, sums):
        @pl.when(i + 1 < tiles)
        def _():
            g_load(i + 1).start()

        g_load(i).wait()
        base = pl.multiple_of((i % 2) * tile, tile)
        dest = pl.multiple_of(i * tile, tile)

        def split_strip(j, total):
            col = pl.ds(pl.multiple_of(j * strip, strip), strip)
            x = stage[pl.ds(base, tile), col]
            hi = x.astype(jnp.bfloat16)
            ghi[pl.ds(dest, tile), col] = hi
            glo[pl.ds(dest, tile), col] = (x - hi.astype(jnp.float32)).astype(jnp.bfloat16)
            xx = x * x
            for lane in range(0, strip, 128):
                total = total + xx[:, lane:lane + 128]
            return total

        total = lax.fori_loop(0, width // strip, split_strip, jnp.zeros((tile, 128), jnp.float32))
        row = jnp.sum(total.T, axis=0, keepdims=True)
        sq_own[:, pl.ds(dest, tile)] = jnp.broadcast_to(row, (8, tile))
        return sums

    lax.fori_loop(0, tiles, split_tile, 0)
    for k in range(1, n_co):
        sq_copy(k).start()

    depth = min(2048, width)
    block = 256
    count = n_ex * rows

    def load(off, side, s):
        origin = device_at(off)
        if side:
            origin = origin + 1 - 2 * core
        src = own_rows(s) if off == 0 and not side else buf.at[s, origin]
        return pltpu.make_async_copy(
            src,
            stage.at[pl.ds(pl.multiple_of(origin * rows, rows), rows)],
            load_sem.at[2 + off * 2 + side],
        )

    def compute(s):
        for off in range(chips):
            load(off, 0, s).start()
        for off in range(chips):
            sibling_copy(off, s, True).wait_recv()
            load(off, 1, s).start()
        for off in range(chips):
            load(off, 0, s).wait()
            load(off, 1, s).wait()

        def split_queries(j, c):
            col = pl.ds(pl.multiple_of(j * strip, strip), strip)
            x = stage[:, col] * scale_ref[:, col]
            hi = x.astype(jnp.bfloat16)
            qhi[:, col] = hi
            qlo[:, col] = (x - hi.astype(jnp.float32)).astype(jnp.bfloat16)
            return c

        lax.fori_loop(0, width // strip, split_queries, 0)

        def block_scores(b, c):
            ex_rows = pl.ds(pl.multiple_of(b * block, block), block)

            def deepen(j, acc):
                col = pl.ds(pl.multiple_of(j * depth, depth), depth)
                a_hi, b_hi = qhi[:, col], ghi[ex_rows, col]
                dot = functools.partial(
                    lax.dot_general, dimension_numbers=CONTRACT_LAST, preferred_element_type=jnp.float32
                )
                small = dot(qlo[:, col], b_hi) + dot(a_hi, glo[ex_rows, col])
                return acc + (small + dot(a_hi, b_hi))

            acc = lax.fori_loop(0, width // depth, deepen, jnp.zeros((count, block), jnp.float32))
            part[s, :, ex_rows] = acc
            return c

        lax.fori_loop(0, examples // block, block_scores, 0)
        for k in range(1, n_co):
            part_copy(k, s, False).start()

    def step(t, c):
        for d in range(1, half + 1):
            s = t - (d - 1)

            @pl.when((s >= 0) & (s < pieces))
            def _():
                ring_copy(0, d, s, True).wait_recv()
                if d < half:
                    ring_copy(0, d + 1, s, False).start()
                ring_copy(1, d, s, True).wait_recv()
                if d < half:
                    ring_copy(1, d + 1, s, False).start()
                if d == 1:
                    @pl.when(s + 2 < pieces)
                    def _():
                        send_own(s + 2)
                sibling_copy(chips - d, s, False).start()
                if d < half:
                    sibling_copy(d, s, False).start()

        s = t - (half - 1)

        @pl.when((s >= 0) & (s < pieces))
        def _():
            compute(s)

        return c

    lax.fori_loop(0, pieces + half - 1, step, 0)

    for k in range(1, n_co):
        sq_copy(k).wait_recv()
    squares = sq_own[...]
    for k in range(1, n_co):
        squares = squares + sq_got[k - 1]
    inverse_norm = lax.rsqrt(squares[0:1] + epsilon)

    def finish(s, c):
        for k in range(1, n_co):
            part_copy(k, s, True).wait_recv()
        total = part[s, pl.ds(pl.multiple_of(co * owned, owned), owned)]
        for k in range(1, n_co):
            total = total + got[k - 1, s]
        total = total * inverse_norm
        for i in range(n_ex // n_co):
            at = pl.multiple_of(i * rows * pieces + s * rows, rows)
            out_ref[pl.ds(at, rows), :] = total[i * rows:(i + 1) * rows]
        return c

    lax.fori_loop(0, pieces, finish, 0)

    def drain(s, c):
        for way in range(2):
            for d in range(1, half + 1):
                ring_copy(way, d, s, False).wait_send()
        for off in range(chips):
            sibling_copy(off, s, False).wait_send()
        for k in range(1, n_co):
            part_copy(k, s, False).wait_send()
        return c

    lax.fori_loop(0, pieces, drain, 0)
    for k in range(1, n_co):
        sq_copy(k).wait_send()


def shards(n_ex, n_co, train_grads, queries, module_ids, module_scale, example_ids):
    examples, width = train_grads.shape
    position = lax.axis_index("co") * width + lax.iota(jnp.int32, width)
    table_index = lax.iota(jnp.int32, module_scale.shape[0])
    picked = jnp.sum(
        jnp.where(module_ids[:, None] == table_index[None, :], module_scale[None, :], 0.0), axis=1
    )
    window_index = lax.iota(jnp.int32, module_ids.shape[0])
    coord_scale = jnp.sum(
        jnp.where((position // PROJ)[:, None] == window_index[None, :], picked[None, :], 0.0), axis=1
    )

    chips = n_ex // 2
    pieces = PIECES
    rows = queries.shape[0] // pieces
    count = n_ex * rows
    owned = (n_ex // n_co) * rows
    f32, bf16 = jnp.float32, jnp.bfloat16
    dma = pltpu.SemaphoreType.DMA
    normed, _ = pl.pallas_call(
        functools.partial(kernel, n_ex, n_co, pieces),
        out_shape=(
            jax.ShapeDtypeStruct((owned * pieces, examples), f32),
            jax.ShapeDtypeStruct((pieces, n_ex, rows, width), f32),
        ),
        in_specs=[
            pl.BlockSpec(memory_space=pl.ANY),
            pl.BlockSpec(memory_space=pl.ANY),
            pl.BlockSpec(memory_space=pltpu.VMEM),
        ],
        out_specs=(pl.BlockSpec(memory_space=pltpu.VMEM), pl.BlockSpec(memory_space=pl.ANY)),
        scratch_shapes=[
            pltpu.VMEM((examples, width), bf16),
            pltpu.VMEM((examples, width), bf16),
            pltpu.VMEM((count, width), f32),
            pltpu.VMEM((count, width), bf16),
            pltpu.VMEM((count, width), bf16),
            pltpu.VMEM((pieces, count, examples), f32),
            pltpu.VMEM((n_co - 1, pieces, owned, examples), f32),
            pltpu.VMEM((8, examples), f32),
            pltpu.VMEM((n_co - 1, 8, examples), f32),
            dma((2, chips // 2, pieces)),
            dma((2, chips // 2, pieces)),
            dma((chips, pieces)),
            dma((chips, pieces)),
            dma((n_co - 1, pieces)),
            dma((n_co - 1, pieces)),
            dma((n_co - 1,)),
            dma((n_co - 1,)),
            dma((2 + n_ex,)),
        ],
        compiler_params=pltpu.CompilerParams(
            collective_id=0, has_side_effects=True, vmem_limit_bytes=67043328
        ),
    )(queries, train_grads, coord_scale[None, :])

    local_ids = example_ids - lax.axis_index("ex") * examples
    place = (local_ids[:, None] == lax.iota(jnp.int32, examples)[None, :]).astype(f32)
    return lax.dot_general(
        normed, place, (((1,), (0,)), ((), ())), precision=lax.Precision.HIGHEST, preferred_element_type=f32
    )


def solution(mesh):
    return jax.shard_map(
        functools.partial(shards, mesh.shape["ex"], mesh.shape["co"]),
        mesh=mesh,
        in_specs=(P("ex", "co"), P("ex", "co"), P(), P(), P("ex")),
        out_specs=P("co", "ex"),
        check_vma=False,
    )
```

```python
import functools

import jax
import jax.numpy as jnp
from jax import lax
from jax.experimental import pallas as pl
from jax.experimental.pallas import tpu as pltpu
from jax.sharding import PartitionSpec as P

PROJ = 4096
MESH = pl.DeviceIdType.MESH
PIECES = 8
LEAD = 2
CONTRACT_LAST = (((1,), (1,)), ((), ()))

epsilon = 1e-06


def kernel(n_ex, n_co, pieces, q_ref, g_ref, scale_ref, out_ref, buf,
           ghi, glo, fresh, stage, split, part, got, sq_own, sq_got,
           ring_send, ring_recv, sib_send, sib_recv, part_send, part_recv, sq_send, sq_recv, load_sem):
    chips = n_ex // 2
    half = chips // 2
    ex = lax.axis_index("ex")
    co = lax.axis_index("co")
    core = ex % 2

    def snake(pos):
        upper = pos // half
        return pos * (1 - upper) + upper * (half + chips - 1 - pos)

    pos = snake(ex // 2)

    def device_at(step):
        return snake((pos + step + chips) % chips) * 2 + core

    right = device_at(1)
    left = device_at(-1)
    sibling = ex + 1 - 2 * core
    rows = q_ref.shape[0] // pieces
    width = q_ref.shape[1]
    mid = width // 2
    examples = g_ref.shape[0]
    owned = (n_ex // n_co) * rows

    barrier = pltpu.get_barrier_semaphore()
    for other in (right, left, sibling):
        pl.semaphore_signal(barrier, inc=1, device_id={"ex": other}, device_id_type=MESH)
    for k in range(1, n_co):
        pl.semaphore_signal(barrier, inc=1, device_id={"co": (co + k) % n_co}, device_id_type=MESH)
    pl.semaphore_wait(barrier, 3 + n_co - 1)

    def own_rows(s):
        return q_ref.at[pl.ds(pl.multiple_of(s * rows, rows), rows)]

    def ring_copy(way, d, s, arriving):
        back = d if arriving else d - 1
        origin = device_at(-back if way == 0 else back)
        if d == half and half > 1:
            span = pl.ds(way * mid, mid)
        else:
            span = pl.ds(0, width)
        if d == 1 and not arriving:
            src = own_rows(s)
        else:
            src = buf.at[s, origin, :, span]
        return pltpu.make_async_remote_copy(
            src_ref=src,
            dst_ref=buf.at[s, origin, :, span],
            send_sem=ring_send.at[way, d - 1, s],
            recv_sem=ring_recv.at[way, d - 1, s],
            device_id={"ex": right if way == 0 else left},
            device_id_type=MESH,
        )

    def sibling_copy(off, s, arriving):
        origin = device_at(off)
        if arriving:
            origin = origin + 1 - 2 * core
        src = own_rows(s) if off == 0 and not arriving else buf.at[s, origin]
        return pltpu.make_async_remote_copy(
            src_ref=src,
            dst_ref=buf.at[s, origin],
            send_sem=sib_send.at[off, s],
            recv_sem=sib_recv.at[off, s],
            device_id={"ex": sibling},
            device_id_type=MESH,
        )

    block = 256
    blocks = examples // block

    def part_copy(k, s, b):
        owner = (co + k) % n_co
        cols = pl.ds(pl.multiple_of(b * block, block), block)
        return pltpu.make_async_remote_copy(
            src_ref=part.at[s, pl.ds(pl.multiple_of(owner * owned, owned), owned), cols],
            dst_ref=got.at[k - 1, s, :, cols],
            send_sem=part_send.at[k - 1, s, b],
            recv_sem=part_recv.at[k - 1, s, b],
            device_id={"co": owner},
            device_id_type=MESH,
        )

    def sq_copy(k):
        return pltpu.make_async_remote_copy(
            src_ref=sq_own,
            dst_ref=sq_got.at[k - 1],
            send_sem=sq_send.at[k - 1],
            recv_sem=sq_recv.at[k - 1],
            device_id={"co": (co + k) % n_co},
            device_id_type=MESH,
        )

    def send_own(s):
        ring_copy(0, 1, s, False).start()
        ring_copy(1, 1, s, False).start()
        sibling_copy(0, s, False).start()

    for s in range(min(LEAD, pieces)):
        send_own(s)

    tile = fresh.shape[1]
    tiles = examples // tile
    strip = min(512, width)

    def g_load(i):
        slot = i % 2
        return pltpu.make_async_copy(
            g_ref.at[pl.ds(pl.multiple_of(i * tile, tile), tile)],
            fresh.at[slot],
            load_sem.at[slot],
        )

    g_load(0).start()

    def split_tile(i, sums):
        @pl.when(i + 1 < tiles)
        def _():
            g_load(i + 1).start()

        g_load(i).wait()
        slot = i % 2
        dest = pl.multiple_of(i * tile, tile)

        def split_strip(j, total):
            col = pl.ds(pl.multiple_of(j * strip, strip), strip)
            x = fresh[slot, :, col]
            hi = x.astype(jnp.bfloat16)
            ghi[pl.ds(dest, tile), col] = hi
            glo[pl.ds(dest, tile), col] = (x - hi.astype(jnp.float32)).astype(jnp.bfloat16)
            xx = x * x
            for lane in range(0, strip, 128):
                total = total + xx[:, lane:lane + 128]
            return total

        total = lax.fori_loop(0, width // strip, split_strip, jnp.zeros((tile, 128), jnp.float32))
        row = jnp.sum(total.T, axis=0, keepdims=True)
        sq_own[:, pl.ds(dest, tile)] = jnp.broadcast_to(row, (8, tile))
        return sums

    lax.fori_loop(0, tiles, split_tile, 0)
    for k in range(1, n_co):
        sq_copy(k).start()

    depth = min(8192, width)
    count = n_ex * rows

    def load(off, side, s):
        origin = device_at(off)
        if side:
            origin = origin + 1 - 2 * core
        src = own_rows(s) if off == 0 and not side else buf.at[s, origin]
        return pltpu.make_async_copy(
            src,
            stage.at[pl.ds(pl.multiple_of(origin * rows, rows), rows)],
            load_sem.at[2 + off * 2 + side],
        )

    def compute(s):
        for off in range(chips):
            load(off, 0, s).start()
        for off in range(chips):
            sibling_copy(off, s, True).wait_recv()
            load(off, 1, s).start()
        for off in range(chips):
            load(off, 0, s).wait()
            load(off, 1, s).wait()

        def split_queries(j, c):
            col = pl.ds(pl.multiple_of(j * strip, strip), strip)
            x = stage[:, col] * scale_ref[:, col]
            hi = x.astype(jnp.bfloat16)
            split[pl.ds(0, count), col] = hi
            split[pl.ds(count, count), col] = (x - hi.astype(jnp.float32)).astype(jnp.bfloat16)
            return c

        lax.fori_loop(0, width // strip, split_queries, 0)

        def block_scores(b, c):
            ex_rows = pl.ds(pl.multiple_of(b * block, block), block)

            def deepen(j, acc):
                col = pl.ds(pl.multiple_of(j * depth, depth), depth)
                dot = functools.partial(
                    lax.dot_general, dimension_numbers=CONTRACT_LAST, preferred_element_type=jnp.float32
                )
                both = dot(split[:, col], ghi[ex_rows, col])
                small = both[count:] + dot(split[:count, col], glo[ex_rows, col])
                return acc + (small + both[:count])

            acc = lax.fori_loop(0, width // depth, deepen, jnp.zeros((count, block), jnp.float32))
            part[s, :, ex_rows] = acc
            for k in range(1, n_co):
                part_copy(k, s, b).start()
            return c

        lax.fori_loop(0, blocks, block_scores, 0)

    def step(t, c):
        for d in range(1, half + 1):
            s = t - (d - 1)

            @pl.when((s >= 0) & (s < pieces))
            def _():
                ring_copy(0, d, s, True).wait_recv()
                if d < half:
                    ring_copy(0, d + 1, s, False).start()
                ring_copy(1, d, s, True).wait_recv()
                if d < half:
                    ring_copy(1, d + 1, s, False).start()
                if d == 1:
                    @pl.when(s + LEAD < pieces)
                    def _():
                        send_own(s + LEAD)
                sibling_copy(chips - d, s, False).start()
                if d < half:
                    sibling_copy(d, s, False).start()

        s = t - (half - 1)

        @pl.when((s >= 0) & (s < pieces))
        def _():
            compute(s)

        return c

    lax.fori_loop(0, pieces + half - 1, step, 0)

    for k in range(1, n_co):
        sq_copy(k).wait_recv()
    squares = sq_own[...]
    for k in range(1, n_co):
        squares = squares + sq_got[k - 1]
    inverse_norm = lax.rsqrt(squares[0:1] + epsilon)

    def finish(s, c):
        for k in range(1, n_co):
            for b in range(blocks):
                part_copy(k, s, b).wait_recv()
        total = part[s, pl.ds(pl.multiple_of(co * owned, owned), owned)]
        for k in range(1, n_co):
            total = total + got[k - 1, s]
        total = total * inverse_norm
        for i in range(n_ex // n_co):
            at = pl.multiple_of(i * rows * pieces + s * rows, rows)
            out_ref[pl.ds(at, rows), :] = total[i * rows:(i + 1) * rows]
        return c

    lax.fori_loop(0, pieces, finish, 0)

    def drain(s, c):
        for way in range(2):
            for d in range(1, half + 1):
                ring_copy(way, d, s, False).wait_send()
        for off in range(chips):
            sibling_copy(off, s, False).wait_send()
        for k in range(1, n_co):
            for b in range(blocks):
                part_copy(k, s, b).wait_send()
        return c

    lax.fori_loop(0, pieces, drain, 0)
    for k in range(1, n_co):
        sq_copy(k).wait_send()


def shards(n_ex, n_co, train_grads, queries, module_ids, module_scale, example_ids):
    examples, width = train_grads.shape
    position = lax.axis_index("co") * width + lax.iota(jnp.int32, width)
    table_index = lax.iota(jnp.int32, module_scale.shape[0])
    picked = jnp.sum(
        jnp.where(module_ids[:, None] == table_index[None, :], module_scale[None, :], 0.0), axis=1
    )
    window_index = lax.iota(jnp.int32, module_ids.shape[0])
    coord_scale = jnp.sum(
        jnp.where((position // PROJ)[:, None] == window_index[None, :], picked[None, :], 0.0), axis=1
    )

    chips = n_ex // 2
    pieces = min(PIECES, queries.shape[0] // 8)
    rows = queries.shape[0] // pieces
    count = n_ex * rows
    owned = (n_ex // n_co) * rows
    f32, bf16 = jnp.float32, jnp.bfloat16
    dma = pltpu.SemaphoreType.DMA
    normed, _ = pl.pallas_call(
        functools.partial(kernel, n_ex, n_co, pieces),
        out_shape=(
            jax.ShapeDtypeStruct((owned * pieces, examples), f32),
            jax.ShapeDtypeStruct((pieces, n_ex, rows, width), f32),
        ),
        in_specs=[
            pl.BlockSpec(memory_space=pl.ANY),
            pl.BlockSpec(memory_space=pl.ANY),
            pl.BlockSpec(memory_space=pltpu.VMEM),
        ],
        out_specs=(pl.BlockSpec(memory_space=pltpu.VMEM), pl.BlockSpec(memory_space=pl.ANY)),
        scratch_shapes=[
            pltpu.VMEM((examples, width), bf16),
            pltpu.VMEM((examples, width), bf16),
            pltpu.VMEM((2, min(128, examples), width), f32),
            pltpu.VMEM((count, width), f32),
            pltpu.VMEM((2 * count, width), bf16),
            pltpu.VMEM((pieces, count, examples), f32),
            pltpu.VMEM((n_co - 1, pieces, owned, examples), f32),
            pltpu.VMEM((8, examples), f32),
            pltpu.VMEM((n_co - 1, 8, examples), f32),
            dma((2, chips // 2, pieces)),
            dma((2, chips // 2, pieces)),
            dma((chips, pieces)),
            dma((chips, pieces)),
            dma((n_co - 1, pieces, examples // 256)),
            dma((n_co - 1, pieces, examples // 256)),
            dma((n_co - 1,)),
            dma((n_co - 1,)),
            dma((2 + n_ex,)),
        ],
        compiler_params=pltpu.CompilerParams(
            collective_id=0, has_side_effects=True, vmem_limit_bytes=67043328
        ),
    )(queries, train_grads, coord_scale[None, :])

    local_ids = example_ids - lax.axis_index("ex") * examples
    place = (local_ids[:, None] == lax.iota(jnp.int32, examples)[None, :]).astype(f32)
    return lax.dot_general(
        normed, place, (((1,), (0,)), ((), ())), precision=lax.Precision.HIGHEST, preferred_element_type=f32
    )


def solution(mesh):
    return jax.shard_map(
        functools.partial(shards, mesh.shape["ex"], mesh.shape["co"]),
        mesh=mesh,
        in_specs=(P("ex", "co"), P("ex", "co"), P(), P(), P("ex")),
        out_specs=P("co", "ex"),
        check_vma=False,
    )
```

```python
import functools

import jax
import jax.numpy as jnp
from jax import lax
from jax.experimental import pallas as pl
from jax.experimental.pallas import tpu as pltpu
from jax.sharding import PartitionSpec as P

PROJ = 4096
MESH = pl.DeviceIdType.MESH
PIECES = 8
LEAD = 2
CONTRACT_LAST = (((1,), (1,)), ((), ()))

epsilon = 1e-06


def kernel(n_ex, n_co, pieces, q_ref, g_ref, scale_ref, out_ref, buf,
           ghi, glo, fresh, stage, split, part, got, sq_own, sq_got,
           ring_send, ring_recv, sib_send, sib_recv, part_send, part_recv, sq_send, sq_recv, load_sem):
    chips = n_ex // 2
    half = chips // 2
    ex = lax.axis_index("ex")
    co = lax.axis_index("co")
    core = ex % 2

    def snake(pos):
        upper = pos // half
        return pos * (1 - upper) + upper * (half + chips - 1 - pos)

    pos = snake(ex // 2)

    def device_at(step):
        return snake((pos + step + chips) % chips) * 2 + core

    right = device_at(1)
    left = device_at(-1)
    sibling = ex + 1 - 2 * core
    rows = q_ref.shape[0] // pieces
    width = q_ref.shape[1]
    mid = width // 2
    examples = g_ref.shape[0]
    owned = (n_ex // n_co) * rows

    barrier = pltpu.get_barrier_semaphore()
    for other in (right, left, sibling):
        pl.semaphore_signal(barrier, inc=1, device_id={"ex": other}, device_id_type=MESH)
    for k in range(1, n_co):
        pl.semaphore_signal(barrier, inc=1, device_id={"co": (co + k) % n_co}, device_id_type=MESH)
    pl.semaphore_wait(barrier, 3 + n_co - 1)

    def own_rows(s):
        return q_ref.at[pl.ds(pl.multiple_of(s * rows, rows), rows)]

    def ring_copy(way, d, s, arriving):
        back = d if arriving else d - 1
        origin = device_at(-back if way == 0 else back)
        if d == half and half > 1:
            span = pl.ds(way * mid, mid)
        else:
            span = pl.ds(0, width)
        if d == 1 and not arriving:
            src = own_rows(s)
        else:
            src = buf.at[s, origin, :, span]
        return pltpu.make_async_remote_copy(
            src_ref=src,
            dst_ref=buf.at[s, origin, :, span],
            send_sem=ring_send.at[way, d - 1, s],
            recv_sem=ring_recv.at[way, d - 1, s],
            device_id={"ex": right if way == 0 else left},
            device_id_type=MESH,
        )

    def sibling_copy(off, s, arriving):
        origin = device_at(off)
        if arriving:
            origin = origin + 1 - 2 * core
        src = own_rows(s) if off == 0 and not arriving else buf.at[s, origin]
        return pltpu.make_async_remote_copy(
            src_ref=src,
            dst_ref=buf.at[s, origin],
            send_sem=sib_send.at[off, s],
            recv_sem=sib_recv.at[off, s],
            device_id={"ex": sibling},
            device_id_type=MESH,
        )

    block = 256
    blocks = examples // block

    def part_copy(k, s, b):
        owner = (co + k) % n_co
        cols = pl.ds(pl.multiple_of(b * block, block), block)
        return pltpu.make_async_remote_copy(
            src_ref=part.at[s, pl.ds(pl.multiple_of(owner * owned, owned), owned), cols],
            dst_ref=got.at[k - 1, s, :, cols],
            send_sem=part_send.at[k - 1, s, b],
            recv_sem=part_recv.at[k - 1, s, b],
            device_id={"co": owner},
            device_id_type=MESH,
        )

    def sq_copy(k):
        return pltpu.make_async_remote_copy(
            src_ref=sq_own,
            dst_ref=sq_got.at[k - 1],
            send_sem=sq_send.at[k - 1],
            recv_sem=sq_recv.at[k - 1],
            device_id={"co": (co + k) % n_co},
            device_id_type=MESH,
        )

    def send_own(s):
        ring_copy(0, 1, s, False).start()
        ring_copy(1, 1, s, False).start()
        sibling_copy(0, s, False).start()

    for s in range(min(LEAD, pieces)):
        send_own(s)

    def relay(t):
        for d in range(1, half + 1):
            s = t - (d - 1)

            @pl.when((s >= 0) & (s < pieces))
            def _():
                ring_copy(0, d, s, True).wait_recv()
                if d < half:
                    ring_copy(0, d + 1, s, False).start()
                ring_copy(1, d, s, True).wait_recv()
                if d < half:
                    ring_copy(1, d + 1, s, False).start()
                if d == 1:
                    @pl.when(s + LEAD < pieces)
                    def _():
                        send_own(s + LEAD)
                sibling_copy(chips - d, s, False).start()
                if d < half:
                    sibling_copy(d, s, False).start()

    tile = fresh.shape[1]
    tiles = examples // tile
    strip = min(512, width)

    def g_load(i):
        slot = i % 2
        return pltpu.make_async_copy(
            g_ref.at[pl.ds(pl.multiple_of(i * tile, tile), tile)],
            fresh.at[slot],
            load_sem.at[slot],
        )

    g_load(0).start()

    def split_tile(i, sums):
        @pl.when(i + 1 < tiles)
        def _():
            g_load(i + 1).start()

        @pl.when(i == tiles // 2)
        def _():
            relay(0)

        g_load(i).wait()
        slot = i % 2
        dest = pl.multiple_of(i * tile, tile)

        def split_strip(j, total):
            col = pl.ds(pl.multiple_of(j * strip, strip), strip)
            x = fresh[slot, :, col]
            hi = x.astype(jnp.bfloat16)
            ghi[pl.ds(dest, tile), col] = hi
            glo[pl.ds(dest, tile), col] = (x - hi.astype(jnp.float32)).astype(jnp.bfloat16)
            xx = x * x
            for lane in range(0, strip, 128):
                total = total + xx[:, lane:lane + 128]
            return total

        total = lax.fori_loop(0, width // strip, split_strip, jnp.zeros((tile, 128), jnp.float32))
        row = jnp.sum(total.T, axis=0, keepdims=True)
        sq_own[:, pl.ds(dest, tile)] = jnp.broadcast_to(row, (8, tile))
        return sums

    lax.fori_loop(0, tiles, split_tile, 0)
    for k in range(1, n_co):
        sq_copy(k).start()

    depth = min(8192, width)
    count = n_ex * rows

    def load(off, side, s):
        origin = device_at(off)
        if side:
            origin = origin + 1 - 2 * core
        src = own_rows(s) if off == 0 and not side else buf.at[s, origin]
        return pltpu.make_async_copy(
            src,
            stage.at[pl.ds(pl.multiple_of(origin * rows, rows), rows)],
            load_sem.at[2 + off * 2 + side],
        )

    def compute(s):
        for off in range(chips):
            load(off, 0, s).start()
        for off in range(chips):
            sibling_copy(off, s, True).wait_recv()
            load(off, 1, s).start()
        for off in range(chips):
            load(off, 0, s).wait()
            load(off, 1, s).wait()

        def split_queries(j, c):
            col = pl.ds(pl.multiple_of(j * strip, strip), strip)
            x = stage[:, col] * scale_ref[:, col]
            hi = x.astype(jnp.bfloat16)
            split[pl.ds(0, count), col] = hi
            split[pl.ds(count, count), col] = (x - hi.astype(jnp.float32)).astype(jnp.bfloat16)
            return c

        lax.fori_loop(0, width // strip, split_queries, 0)

        def block_scores(b, c):
            ex_rows = pl.ds(pl.multiple_of(b * block, block), block)

            def deepen(j, acc):
                col = pl.ds(pl.multiple_of(j * depth, depth), depth)
                dot = functools.partial(
                    lax.dot_general, dimension_numbers=CONTRACT_LAST, preferred_element_type=jnp.float32
                )
                both = dot(split[:, col], ghi[ex_rows, col])
                small = both[count:] + dot(split[:count, col], glo[ex_rows, col])
                return acc + (small + both[:count])

            acc = lax.fori_loop(0, width // depth, deepen, jnp.zeros((count, block), jnp.float32))
            part[s, :, ex_rows] = acc
            for k in range(1, n_co):
                part_copy(k, s, b).start()
            return c

        lax.fori_loop(0, blocks, block_scores, 0)

    def step(t, c):
        @pl.when(t > 0)
        def _():
            relay(t)

        s = t - (half - 1)

        @pl.when((s >= 0) & (s < pieces))
        def _():
            compute(s)

        return c

    lax.fori_loop(0, pieces + half - 1, step, 0)

    for k in range(1, n_co):
        sq_copy(k).wait_recv()
    squares = sq_own[...]
    for k in range(1, n_co):
        squares = squares + sq_got[k - 1]
    inverse_norm = lax.rsqrt(squares[0:1] + epsilon)

    def finish(s, c):
        for k in range(1, n_co):
            for b in range(blocks):
                part_copy(k, s, b).wait_recv()
        total = part[s, pl.ds(pl.multiple_of(co * owned, owned), owned)]
        for k in range(1, n_co):
            total = total + got[k - 1, s]
        total = total * inverse_norm
        for i in range(n_ex // n_co):
            at = pl.multiple_of(i * rows * pieces + s * rows, rows)
            out_ref[pl.ds(at, rows), :] = total[i * rows:(i + 1) * rows]
        return c

    lax.fori_loop(0, pieces, finish, 0)

    def drain(s, c):
        for way in range(2):
            for d in range(1, half + 1):
                ring_copy(way, d, s, False).wait_send()
        for off in range(chips):
            sibling_copy(off, s, False).wait_send()
        for k in range(1, n_co):
            for b in range(blocks):
                part_copy(k, s, b).wait_send()
        return c

    lax.fori_loop(0, pieces, drain, 0)
    for k in range(1, n_co):
        sq_copy(k).wait_send()


def shards(n_ex, n_co, train_grads, queries, module_ids, module_scale, example_ids):
    examples, width = train_grads.shape
    position = lax.axis_index("co") * width + lax.iota(jnp.int32, width)
    table_index = lax.iota(jnp.int32, module_scale.shape[0])
    picked = jnp.sum(
        jnp.where(module_ids[:, None] == table_index[None, :], module_scale[None, :], 0.0), axis=1
    )
    window_index = lax.iota(jnp.int32, module_ids.shape[0])
    coord_scale = jnp.sum(
        jnp.where((position // PROJ)[:, None] == window_index[None, :], picked[None, :], 0.0), axis=1
    )

    chips = n_ex // 2
    pieces = min(PIECES, queries.shape[0] // 8)
    rows = queries.shape[0] // pieces
    count = n_ex * rows
    owned = (n_ex // n_co) * rows
    f32, bf16 = jnp.float32, jnp.bfloat16
    dma = pltpu.SemaphoreType.DMA
    normed, _ = pl.pallas_call(
        functools.partial(kernel, n_ex, n_co, pieces),
        out_shape=(
            jax.ShapeDtypeStruct((owned * pieces, examples), f32),
            jax.ShapeDtypeStruct((pieces, n_ex, rows, width), f32),
        ),
        in_specs=[
            pl.BlockSpec(memory_space=pl.ANY),
            pl.BlockSpec(memory_space=pl.ANY),
            pl.BlockSpec(memory_space=pltpu.VMEM),
        ],
        out_specs=(pl.BlockSpec(memory_space=pltpu.VMEM), pl.BlockSpec(memory_space=pl.ANY)),
        scratch_shapes=[
            pltpu.VMEM((examples, width), bf16),
            pltpu.VMEM((examples, width), bf16),
            pltpu.VMEM((2, min(128, examples), width), f32),
            pltpu.VMEM((count, width), f32),
            pltpu.VMEM((2 * count, width), bf16),
            pltpu.VMEM((pieces, count, examples), f32),
            pltpu.VMEM((n_co - 1, pieces, owned, examples), f32),
            pltpu.VMEM((8, examples), f32),
            pltpu.VMEM((n_co - 1, 8, examples), f32),
            dma((2, chips // 2, pieces)),
            dma((2, chips // 2, pieces)),
            dma((chips, pieces)),
            dma((chips, pieces)),
            dma((n_co - 1, pieces, examples // 256)),
            dma((n_co - 1, pieces, examples // 256)),
            dma((n_co - 1,)),
            dma((n_co - 1,)),
            dma((2 + n_ex,)),
        ],
        compiler_params=pltpu.CompilerParams(
            collective_id=0, has_side_effects=True, vmem_limit_bytes=67043328
        ),
    )(queries, train_grads, coord_scale[None, :])

    local_ids = example_ids - lax.axis_index("ex") * examples
    place = (local_ids[:, None] == lax.iota(jnp.int32, examples)[None, :]).astype(f32)
    return lax.dot_general(
        normed, place, (((1,), (0,)), ((), ())), precision=lax.Precision.HIGH, preferred_element_type=f32
    )


def solution(mesh):
    return jax.shard_map(
        functools.partial(shards, mesh.shape["ex"], mesh.shape["co"]),
        mesh=mesh,
        in_specs=(P("ex", "co"), P("ex", "co"), P(), P(), P("ex")),
        out_specs=P("co", "ex"),
        check_vma=False,
    )
```
